32 devices in a mesh: tile: 8 (over z, y), hidden: 4 (over x, core).
Axes of the slice: x: 2, y: 2, z: 4, core: 2. Of those that a mesh axis runs over, the one named last changes fastest.
Arguments:
- cells: bfloat16 [128, 48, 48, 128], P(('tile', 'hidden')), may hold values from -6 to 6
- partner_edge: int32 [128, 4], P(('tile', 'hidden')), may hold values from 0 to 511, as said below
- edge_flip: int32 [128, 4], P(('tile', 'hidden')), may hold values from 0 to 1, as said below
- dw_weight: float32 [9, 128], replicated, may hold values from -2 to 2
- dw_bias: float32 [128], replicated, may hold values from -3 to 3
- ln_gain: float32 [128], replicated, may hold values from 0.5 to 1.5
- ln_bias: float32 [128], replicated, may hold values from -3 to 3
- w_in: bfloat16 [512, 128], replicated, may hold values from -0.5 to 0.5
- b_in: bfloat16 [512], replicated, may hold values from -3 to 3
- w_out: bfloat16 [512, 128], replicated, may hold values from -0.25 to 0.25
- b_out: float32 [128], replicated, may hold values from -3 to 3
- layer_scale: float32 [128], replicated, may hold values from 0.5 to 1.5
Outputs:
- updated: bfloat16 [128, 48, 48, 128], P(('tile', 'hidden'))
The draws below stay inside these ranges and needn't reach their ends.
Inputs may be any that keep to these rules, and one draw needn't show every extreme that they name: `partner_edge`: edges are matched in pairs: if edge a names edge b, then b names a, a != b, and both carry the same edge_flip. Every edge's partner lies on the same device as its tile or on the device just before or just after it in the order of tile+hidden, the last and the first being neighbours; exactly 4 edges of each device have partners on the next device. `edge_flip`: equal at the two edges of a matched pair.
All inputs are finite; a program needn't handle non-finite values.
Results may differ from the reference program's by a relative error of at most 0.0044.
Values may be sent and summed in bfloat16 or wider, within the bound.
A program may use at most 64 MiB of HBM per device.

```python
import jax
import jax.numpy as jnp
from jax import lax

C = 128
FFN = 512
TS = 48
TPD = 4
TILES = 128


def matching(key):
    base_key = jax.random.fold_in(key, 7)
    groups = TILES // TPD
    edge_count = 4 * TPD
    device_keys = jax.random.split(base_key, groups)
    orders = jax.vmap(lambda one_key: jax.random.permutation(one_key, edge_count))(device_keys)
    offsets = (jnp.arange(groups, dtype=jnp.int32) * edge_count)[:, None]
    going_right = orders[:, :TPD] + offsets
    going_left = orders[:, TPD:2 * TPD] + offsets
    left_next = jnp.roll(going_left, -1, axis=0)
    inner_edges = orders[:, 2 * TPD:] + offsets
    first_inner = inner_edges[:, 0::2]
    second_inner = inner_edges[:, 1::2]
    sources = jnp.concatenate([going_right.ravel(), left_next.ravel(), first_inner.ravel(), second_inner.ravel()])
    targets = jnp.concatenate([left_next.ravel(), going_right.ravel(), second_inner.ravel(), first_inner.ravel()])
    flip_key = jax.random.fold_in(base_key, 11)
    cross_flip = jax.random.randint(jax.random.fold_in(flip_key, 1), (groups * TPD,), 0, 2, dtype=jnp.int32)
    inner_flip = jax.random.randint(jax.random.fold_in(flip_key, 2), (groups * TPD,), 0, 2, dtype=jnp.int32)
    flip_values = jnp.concatenate([cross_flip, cross_flip, inner_flip, inner_flip])
    partner = jnp.zeros((groups * edge_count,), jnp.int32).at[sources].set(targets.astype(jnp.int32))
    flipped = jnp.zeros((groups * edge_count,), jnp.int32).at[sources].set(flip_values)
    return (partner.reshape(TILES, 4), flipped.reshape(TILES, 4))


def draw_partner_edge(key, part):
    return matching(key)[0]


def draw_edge_flip(key, part):
    return matching(key)[1]


def block_scale(stream_key, dims, pieces, least, largest):
    level, own = 1.0, jax.random.fold_in(stream_key, 6)
    for dim, shards_of in pieces:
        draws = jnp.exp(jax.random.uniform(jax.random.fold_in(own, dim), (shards_of,), jnp.float32, least / len(pieces), largest / len(pieces)))
        level = level * jnp.repeat(draws, dims[dim] // shards_of).reshape([-1 if axis == dim else 1 for axis in range(len(dims))])
    return level


def gaussian(own_key, extent, width, limit, cuts=(), kind=jnp.bfloat16):
    level = block_scale(own_key, extent, cuts, -0.22, 0.18) if cuts else 1.0
    entries = jax.random.normal(own_key, extent, jnp.float32) * width * level
    return jnp.minimum(jnp.maximum(entries, -limit), limit).astype(kind)


def setup_inputs(seed: int = 0) -> dict:
    key_list = jax.random.split(jax.random.key(seed), 13)
    return {
        "cells": gaussian(key_list[0], (TILES, TS, TS, C), 1.0, 6.0, ((0, 32),)),
        "partner_edge": draw_partner_edge(jax.random.fold_in(key_list[12], 71), 0),
        "edge_flip": draw_edge_flip(jax.random.fold_in(key_list[12], 71), 0),
        "dw_weight": gaussian(key_list[3], (9, C), 9 ** -0.5, 2.0, (), jnp.float32),
        "dw_bias": gaussian(key_list[4], (C,), 0.5, 3.0, (), jnp.float32),
        "ln_gain": jnp.clip(1.0 + 0.1 * jax.random.normal(key_list[5], (C,), jnp.float32), 0.5, 1.5),
        "ln_bias": gaussian(key_list[6], (C,), 0.5, 3.0, (), jnp.float32),
        "w_in": gaussian(key_list[7], (FFN, C), C ** -0.5, 0.5),
        "b_in": gaussian(key_list[8], (FFN,), 0.5, 3.0),
        "w_out": gaussian(key_list[9], (FFN, C), FFN ** -0.5, 0.25),
        "b_out": gaussian(key_list[10], (C,), 0.5, 3.0, (), jnp.float32),
        "layer_scale": jnp.clip(jax.random.uniform(key_list[11], (C,), jnp.float32, 0.5, 1.5), 0.5, 1.5),
    }


def boundary(tiles_in):
    return jnp.stack([tiles_in[:, 0], tiles_in[:, :, -1], tiles_in[:, -1], tiles_in[:, :, 0]], axis=1)

def pad_tiles(tiles_in, halo_rows):
    north_rim = halo_rows[:, 0].astype(jnp.float32)
    east_rim = halo_rows[:, 1].astype(jnp.float32)
    south_rim = halo_rows[:, 2].astype(jnp.float32)
    west_rim = halo_rows[:, 3].astype(jnp.float32)
    top_row = jnp.concatenate([0.5 * (north_rim[:, :1] + west_rim[:, :1]), north_rim, 0.5 * (north_rim[:, -1:] + east_rim[:, :1])], axis=1)
    bottom_row = jnp.concatenate([0.5 * (south_rim[:, :1] + west_rim[:, -1:]), south_rim, 0.5 * (south_rim[:, -1:] + east_rim[:, -1:])], axis=1)
    middle = jnp.concatenate([west_rim[:, :, None], tiles_in.astype(jnp.float32), east_rim[:, :, None]], axis=2)
    return jnp.concatenate([top_row[:, None], middle, bottom_row[:, None]], axis=1)

def depthwise(padded, dw_weight, dw_bias):
    side_len = padded.shape[1] - 2
    total = jnp.zeros(padded[:, 1:-1, 1:-1].shape, jnp.float32) + dw_bias
    for row_tap in range(3):
        for col_tap in range(3):
            total = total + dw_weight[3 * row_tap + col_tap] * padded[:, row_tap:row_tap + side_len, col_tap:col_tap + side_len]
    return total

def layer_norm(conv, ln_gain, ln_bias):
    center = lax.optimization_barrier(jnp.mean(conv, axis=-1, keepdims=True))
    spread = lax.optimization_barrier(jnp.mean((conv - center) ** 2, axis=-1, keepdims=True))
    return ((conv - center) * lax.rsqrt(spread + 1e-06) * ln_gain + ln_bias).astype(jnp.bfloat16)

def reference(cells, partner_edge, edge_flip, dw_weight, dw_bias, ln_gain, ln_bias, w_in, b_in, w_out, b_out, layer_scale):
    tile_count, tile_side, _, channels = cells.shape
    edge_count = 4 * tile_count
    rims = boundary(cells).reshape(edge_count, tile_side, channels)
    halo_rows = rims[partner_edge.reshape(edge_count)]
    halo_rows = jnp.where(edge_flip.reshape(edge_count)[:, None, None] == 1, halo_rows[:, ::-1], halo_rows)
    halo_rows = halo_rows.reshape(tile_count, 4, tile_side, channels)

    def one_tile(pair):
        tile_in, tile_halo = pair
        padded = pad_tiles(tile_in[None], tile_halo[None])
        conv = depthwise(padded, dw_weight, dw_bias)
        normed = layer_norm(conv, ln_gain, ln_bias).reshape(-1, channels)
        pre = lax.dot_general(normed, w_in, (((1,), (1,)), ((), ())), preferred_element_type=jnp.float32) + b_in.astype(jnp.float32)
        act = jax.nn.gelu(pre, approximate=False).astype(jnp.bfloat16)
        mixed = jnp.dot(act, w_out, preferred_element_type=jnp.float32) + b_out
        mixed = mixed.reshape(tile_side, tile_side, channels)
        return (tile_in.astype(jnp.float32) + layer_scale * mixed).astype(jnp.bfloat16)
    return lax.map(one_tile, (cells, halo_rows))
```

```python
import functools

import jax
import jax.numpy as jnp
from jax import lax
from jax.experimental import pallas as pl
from jax.experimental.pallas import tpu as pltpu
from jax.sharding import PartitionSpec as P

AXES = ("tile", "hidden")
OFF = 8


def shifted(array, by):
    count = lax.axis_size(AXES)
    return lax.ppermute(array, AXES, [(i, (i + by) % count) for i in range(count)])


def boundary(tiles_in):
    return jnp.stack(
        [tiles_in[:, 0], tiles_in[:, :, -1], tiles_in[:, -1], tiles_in[:, :, 0]], axis=1
    )


def block_kernel(
    rows,
    pick_ref,
    flip_ref,
    cells_ref,
    cand_ref,
    dw_ref,
    vec_ref,
    w_in_ref,
    b_in_ref,
    w_out_ref,
    out_ref,
    pad_ref,
):
    side = cells_ref.shape[1]
    channels = cells_ref.shape[3]
    tile = pl.program_id(0)
    pad_ref[pl.ds(1, side), pl.ds(OFF, side), :] = cells_ref[0].astype(jnp.float32)
    r_id = lax.broadcasted_iota(jnp.int32, (side, side), 0)
    c_id = lax.broadcasted_iota(jnp.int32, (side, side), 1)
    lines = []
    for s in range(4):
        edge = tile * 4 + s
        target = jnp.where(flip_ref[edge] == 1, side - 1 - r_id, r_id)
        order = jnp.where(c_id == target, 1.0, 0.0).astype(jnp.bfloat16)
        lines.append(
            jnp.dot(order, cand_ref[pick_ref[edge]], preferred_element_type=jnp.float32)
        )
    north, east, south, west = lines
    pad_ref[0, pl.ds(OFF, side), :] = north
    pad_ref[side + 1, pl.ds(OFF, side), :] = south
    for r in range(side):
        pad_ref[r + 1, OFF - 1 : OFF, :] = west[r : r + 1]
        pad_ref[r + 1, OFF + side : OFF + side + 1, :] = east[r : r + 1]
    pad_ref[0, OFF - 1 : OFF, :] = 0.5 * (north[:1] + west[:1])
    pad_ref[0, OFF + side : OFF + side + 1, :] = 0.5 * (north[-1:] + east[:1])
    pad_ref[side + 1, OFF - 1 : OFF, :] = 0.5 * (south[:1] + west[-1:])
    pad_ref[side + 1, OFF + side : OFF + side + 1, :] = 0.5 * (south[-1:] + east[-1:])

    dw_bias = vec_ref[0:1]
    gain = vec_ref[1:2]
    bias = vec_ref[2:3]
    b_out = vec_ref[3:4]
    scale = vec_ref[4:5]
    b_in = b_in_ref[...].astype(jnp.float32)

    @pl.loop(0, side // rows)
    def _(step):
        base = step * rows
        normed = []
        for r in range(rows):
            total = jnp.broadcast_to(dw_bias, (side, channels))
            for a in range(3):
                for b in range(3):
                    k = 3 * a + b
                    total = total + dw_ref[k : k + 1] * pad_ref[
                        base + r + a, pl.ds(OFF - 1 + b, side), :
                    ]
            center = total - jnp.mean(total, axis=-1, keepdims=True)
            spread = jnp.mean(center * center, axis=-1, keepdims=True)
            value = center * lax.rsqrt(spread + 1e-06) * gain + bias
            normed.append(value.astype(jnp.bfloat16))
        normed = jnp.concatenate(normed, axis=0)
        pre = (
            lax.dot_general(
                normed,
                w_in_ref[...],
                (((1,), (1,)), ((), ())),
                preferred_element_type=jnp.float32,
            )
            + b_in
        )
        half = 0.5 * pre
        act = (half + half * lax.erf(pre * 0.7071067811865476)).astype(jnp.bfloat16)
        mixed = jnp.dot(act, w_out_ref[...], preferred_element_type=jnp.float32) + b_out
        mixed = (scale * mixed).reshape(rows, side, channels)
        old = cells_ref[0, pl.ds(base, rows)].astype(jnp.float32)
        out_ref[0, pl.ds(base, rows)] = (old + mixed).astype(out_ref.dtype)


def per_device(
    cells,
    partner_edge,
    edge_flip,
    dw_weight,
    dw_bias,
    ln_gain,
    ln_bias,
    w_in,
    b_in,
    w_out,
    b_out,
    layer_scale,
):
    tile_count, side, _, channels = cells.shape
    hidden = w_in.shape[0]
    edge_count = 4 * tile_count
    rims = boundary(cells).reshape(edge_count, side, channels)
    devices = lax.axis_size(AXES)
    position = lax.axis_index(AXES)
    flat_partner = partner_edge.reshape(edge_count)
    flat_flip = edge_flip.reshape(edge_count)
    local_edge = flat_partner % edge_count
    distance = jnp.mod(flat_partner // edge_count - position, devices)
    group = jnp.where(distance == devices - 1, 0, jnp.where(distance == 1, 2, 1))
    pick = group * edge_count + local_edge
    before = shifted(rims, 1)
    after = shifted(rims, -1)
    cand = jnp.concatenate([before, rims, after], axis=0)
    vec = jnp.stack([dw_bias, ln_gain, ln_bias, b_out, layer_scale], axis=0)

    def whole(shape):
        return pl.BlockSpec(shape, lambda t, p, f: (0,) * len(shape))

    tile_spec = pl.BlockSpec((1, side, side, channels), lambda t, p, f: (t, 0, 0, 0))
    return pl.pallas_call(
        functools.partial(block_kernel, 4),
        out_shape=jax.ShapeDtypeStruct(cells.shape, jnp.bfloat16),
        grid_spec=pltpu.PrefetchScalarGridSpec(
            num_scalar_prefetch=2,
            grid=(tile_count,),
            in_specs=[
                tile_spec,
                whole(cand.shape),
                whole(dw_weight.shape),
                whole(vec.shape),
                whole(w_in.shape),
                whole((1, hidden)),
                whole(w_out.shape),
            ],
            out_specs=tile_spec,
            scratch_shapes=[pltpu.VMEM((side + 2, side + 2 * OFF, channels), jnp.float32)],
        ),
        name="block",
    )(pick, flat_flip, cells, cand, dw_weight, vec, w_in, b_in.reshape(1, hidden), w_out)


def solution(mesh):
    spread_spec = P(AXES, None, None, None)
    in_specs = (spread_spec, P(AXES, None), P(AXES, None)) + (P(),) * 9
    return jax.shard_map(
        per_device, mesh=mesh, in_specs=in_specs, out_specs=spread_spec, check_vma=False
    )
```

```python
import functools

import jax
import jax.numpy as jnp
from jax import lax
from jax.experimental import pallas as pl
from jax.experimental.pallas import tpu as pltpu
from jax.sharding import PartitionSpec as P

AXES = ("tile", "hidden")
OFF = 8
CELLS_PER_CHUNK = 256
MESH = pl.DeviceIdType.MESH
ROOT_HALF = 0.7071067811865476


def divisor(total, limit):
    return max(d for d in range(1, min(total, limit) + 1) if total % d == 0)


def block_kernel(
    sizes,
    partner_ref,
    flip_ref,
    cells_ref,
    dw_ref,
    dw_bias_ref,
    gain_ref,
    bias_ref,
    w_in_ref,
    b_in_ref,
    w_out_ref,
    b_out_ref,
    scale_ref,
    out_ref,
    cells_buf,
    pad_ref,
    cand_ref,
    w_aug_ref,
    buf_a,
    buf_b,
    load_sem,
    send_sem,
    recv_sem,
):
    tile_devices, hidden_devices = sizes
    tiles, side, _, channels = out_ref.shape
    edges = 4 * tiles
    width = side + 2 * OFF
    devices = tile_devices * hidden_devices
    me = lax.axis_index("tile") * hidden_devices + lax.axis_index("hidden")

    def at(position):
        return (position // hidden_devices, position % hidden_devices)

    right = lax.rem(me + 1, devices)
    left = lax.rem(me + devices - 1, devices)

    loads = [
        pltpu.make_async_copy(cells_ref.at[t], cells_buf.at[t], load_sem.at[t])
        for t in range(tiles)
    ]
    for copy in loads:
        copy.start()
    barrier = pltpu.get_barrier_semaphore()
    for neighbour in (left, right):
        pl.semaphore_signal(barrier, inc=1, device_id=at(neighbour), device_id_type=MESH)

    hidden = w_in_ref.shape[0]
    eye = (
        lax.broadcasted_iota(jnp.int32, (channels, channels), 0)
        == lax.broadcasted_iota(jnp.int32, (channels, channels), 1)
    ).astype(jnp.bfloat16)
    w_aug_ref[0:channels, :] = lax.dot_general(
        eye, w_in_ref[...], (((1,), (1,)), ((), ())), preferred_element_type=jnp.float32
    ).astype(jnp.bfloat16)
    b_in = b_in_ref[...].astype(jnp.float32).reshape(1, hidden) * ROOT_HALF
    b_high = b_in.astype(jnp.bfloat16).astype(jnp.float32)
    row_id = lax.broadcasted_iota(jnp.int32, (channels, hidden), 0)
    extra = jnp.where(row_id == 0, b_high, jnp.where(row_id == 1, b_in - b_high, 0.0))
    w_aug_ref[channels : 2 * channels, :] = extra.astype(jnp.bfloat16)
    lane_id = lax.broadcasted_iota(jnp.int32, (buf_a.shape[0], channels), 1)
    ones = jnp.where(lane_id < 2, 1.0, 0.0).astype(jnp.bfloat16)
    buf_a[:, channels : 2 * channels] = ones
    buf_b[:, channels : 2 * channels] = ones

    flat_pad = pad_ref.reshape(tiles * (side + 2) * width, channels)
    for t in range(tiles):
        loads[t].wait()
        top = t * (side + 2)
        pad_ref[pl.ds(top + 1, side), pl.ds(OFF, side), :] = cells_buf[t].astype(jnp.float32)
        first = (top + 1) * width + OFF
        cand_ref[edges + 4 * t] = cells_buf[t, 0]
        cand_ref[edges + 4 * t + 2] = cells_buf[t, side - 1]
        east = flat_pad[pl.ds(first + side - 1, side, stride=width), :]
        cand_ref[edges + 4 * t + 1] = east.astype(jnp.bfloat16)
        west = flat_pad[pl.ds(first, side, stride=width), :]
        cand_ref[edges + 4 * t + 3] = west.astype(jnp.bfloat16)

    pl.semaphore_wait(barrier, 2)
    own = cand_ref.at[pl.ds(edges, edges)]
    sends = [
        pltpu.make_async_remote_copy(
            src_ref=own,
            dst_ref=cand_ref.at[pl.ds(slot * edges, edges)],
            send_sem=send_sem.at[slot // 2],
            recv_sem=recv_sem.at[slot // 2],
            device_id=at(target),
            device_id_type=MESH,
        )
        for slot, target in ((0, right), (2, left))
    ]
    for copy in sends:
        copy.start()

    dw_bias = dw_bias_ref[...]
    gain = gain_ref[...] * ROOT_HALF
    bias = bias_ref[...] * ROOT_HALF
    out_scale = scale_ref[...] * ROOT_HALF
    out_bias = scale_ref[...] * b_out_ref[...]
    taps = [dw_ref[k : k + 1] for k in range(9)]

    def conv(segments, dst):
        place = 0
        for tile, row, col, count in segments:
            line = tile * (side + 2) + row
            total = jnp.broadcast_to(dw_bias, (count, channels))
            for a in range(3):
                for b in range(3):
                    total = total + taps[3 * a + b] * pad_ref[
                        line + a, pl.ds(OFF - 1 + b + col, count), :
                    ]
            center = total - jnp.mean(total, axis=-1, keepdims=True)
            spread = jnp.mean(center * center, axis=-1, keepdims=True)
            value = center * lax.rsqrt(spread + 1e-06) * gain + bias
            dst[place : place + count, 0:channels] = value.astype(jnp.bfloat16)
            place += count

    def mlp(segments, src):
        z = jnp.dot(src[...], w_aug_ref[...], preferred_element_type=jnp.float32)
        act = (z + z * lax.erf(z)).astype(jnp.bfloat16)
        mixed = jnp.dot(act, w_out_ref[...], preferred_element_type=jnp.float32)
        mixed = mixed * out_scale + out_bias
        place = 0
        for tile, row, col, count in segments:
            line = tile * (side + 2) + row + 1
            old = pad_ref[line, pl.ds(OFF + col, count), :]
            new = old + mixed[place : place + count]
            out_ref[tile, row, pl.ds(col, count), :] = new.astype(out_ref.dtype)
            place += count

    inner_cols = side - 2 * OFF
    inner_rows = side - 2
    rows_in = CELLS_PER_CHUNK // inner_cols
    rows_edge = CELLS_PER_CHUNK // (2 * OFF)

    def inner(chunk):
        found = []
        for k in range(rows_in):
            q = chunk * rows_in + k
            found.append((q // inner_rows, q % inner_rows + 1, OFF, inner_cols))
        return found

    def caps():
        return [(t, r, OFF, inner_cols) for t in range(tiles) for r in (0, side - 1)]

    def sides(chunk):
        found = []
        per_tile = side // rows_edge
        for k in range(rows_edge):
            tile = chunk // per_tile
            row = (chunk % per_tile) * rows_edge + k
            found += [(tile, row, 0, OFF), (tile, row, side - OFF, OFF)]
        return found

    inner_chunks = tiles * inner_rows // rows_in
    side_chunks = tiles * side // rows_edge

    conv(inner(0), buf_a)

    @pl.loop(0, inner_chunks // 2)
    def _(i):
        mlp(inner(2 * i), buf_a)
        conv(inner(2 * i + 1), buf_b)
        mlp(inner(2 * i + 1), buf_b)
        conv(inner(2 * i + 2), buf_a)

    for copy in sends:
        copy.wait()
    r_id = lax.broadcasted_iota(jnp.int32, (side, side), 0)
    c_id = lax.broadcasted_iota(jnp.int32, (side, side), 1)
    for t in range(tiles):
        lines = []
        for s in range(4):
            partner = partner_ref[t, s]
            distance = lax.rem(partner // edges - me + devices, devices)
            group = jnp.where(distance == devices - 1, 0, jnp.where(distance == 1, 2, 1))
            target = jnp.where(flip_ref[t, s] == 1, side - 1 - r_id, r_id)
            order = jnp.where(c_id == target, 1.0, 0.0).astype(jnp.bfloat16)
            line = cand_ref[group * edges + lax.rem(partner, edges)]
            lines.append(jnp.dot(order, line, preferred_element_type=jnp.float32))
        north, east, south, west = lines
        top = t * (side + 2)
        end = top + side + 1
        pad_ref[top, pl.ds(OFF, side), :] = north
        pad_ref[end, pl.ds(OFF, side), :] = south
        first = (top + 1) * width + OFF
        flat_pad[pl.ds(first - 1, side, stride=width), :] = west
        flat_pad[pl.ds(first + side, side, stride=width), :] = east
        pad_ref[top, OFF - 1 : OFF, :] = 0.5 * (north[:1] + west[:1])
        pad_ref[top, OFF + side : OFF + side + 1, :] = 0.5 * (north[-1:] + east[:1])
        pad_ref[end, OFF - 1 : OFF, :] = 0.5 * (south[:1] + west[-1:])
        pad_ref[end, OFF + side : OFF + side + 1, :] = 0.5 * (south[-1:] + east[-1:])

    mlp(inner(inner_chunks - 1), buf_a)
    conv(caps(), buf_b)
    mlp(caps(), buf_b)
    conv(sides(0), buf_a)

    @pl.loop(0, side_chunks // 2 - 1)
    def _(i):
        mlp(sides(2 * i), buf_a)
        conv(sides(2 * i + 1), buf_b)
        mlp(sides(2 * i + 1), buf_b)
        conv(sides(2 * i + 2), buf_a)

    mlp(sides(side_chunks - 2), buf_a)
    conv(sides(side_chunks - 1), buf_b)
    mlp(sides(side_chunks - 1), buf_b)


def per_device(
    sizes,
    cells,
    partner_edge,
    edge_flip,
    dw_weight,
    dw_bias,
    ln_gain,
    ln_bias,
    w_in,
    b_in,
    w_out,
    b_out,
    layer_scale,
):
    tiles, side, _, channels = cells.shape
    hidden = w_in.shape[0]
    edges = 4 * tiles
    vmem = pl.BlockSpec(memory_space=pltpu.VMEM)
    smem = pl.BlockSpec(memory_space=pltpu.SMEM)

    def row(vector):
        return vector.reshape(1, channels)

    return pl.pallas_call(
        functools.partial(block_kernel, sizes),
        out_shape=jax.ShapeDtypeStruct(cells.shape, jnp.bfloat16),
        in_specs=[smem, smem, pl.BlockSpec(memory_space=pl.ANY)] + [vmem] * 9,
        out_specs=vmem,
        scratch_shapes=[
            pltpu.VMEM(cells.shape, jnp.bfloat16),
            pltpu.VMEM((tiles * (side + 2), side + 2 * OFF, channels), jnp.float32),
            pltpu.VMEM((3 * edges, side, channels), jnp.bfloat16),
            pltpu.VMEM((2 * channels, hidden), jnp.bfloat16),
            pltpu.VMEM((CELLS_PER_CHUNK, 2 * channels), jnp.bfloat16),
            pltpu.VMEM((CELLS_PER_CHUNK, 2 * channels), jnp.bfloat16),
            pltpu.SemaphoreType.DMA((tiles,)),
            pltpu.SemaphoreType.DMA((2,)),
            pltpu.SemaphoreType.DMA((2,)),
        ],
        compiler_params=pltpu.CompilerParams(collective_id=0, has_side_effects=True),
        name="block",
    )(
        partner_edge,
        edge_flip,
        cells,
        dw_weight,
        row(dw_bias),
        row(ln_gain),
        row(ln_bias),
        w_in,
        b_in,
        w_out,
        row(b_out),
        row(layer_scale),
    )


def solution(mesh):
    spread_spec = P(AXES, None, None, None)
    in_specs = (spread_spec, P(AXES, None), P(AXES, None)) + (P(),) * 9
    sizes = (mesh.shape["tile"], mesh.shape["hidden"])
    return jax.shard_map(
        functools.partial(per_device, sizes),
        mesh=mesh,
        in_specs=in_specs,
        out_specs=spread_spec,
        check_vma=False,
    )
```

```python
import functools

import jax
import jax.numpy as jnp
from jax import lax
from jax.experimental import pallas as pl
from jax.experimental.pallas import tpu as pltpu
from jax.sharding import PartitionSpec as P

AXES = ("tile", "hidden")
OFF = 8
CELLS_PER_CHUNK = 256
UNROLL = 4
CROSS = 4
GRANT = 32 * 1024 * 1024
MESH = pl.DeviceIdType.MESH
ROOT_HALF = 0.7071067811865476


def tile_of(q, per_tile, tiles):
    tile = 0
    for j in range(1, tiles):
        tile = tile + jnp.where(q >= j * per_tile, 1, 0)
    return tile


def conv(taps, vectors, pad_ref, side, segments, dst):
    dw_bias, gain, bias = vectors
    channels = pad_ref.shape[2]
    start = 0
    for tile, row, col, count in segments:
        line = tile * (side + 2) + row
        total = jnp.broadcast_to(dw_bias, (count, channels))
        for a in range(3):
            for b in range(3):
                total = total + taps[3 * a + b] * pad_ref[
                    line + a, pl.ds(OFF - 1 + b + col, count), :
                ]
        center = total - jnp.mean(total, axis=-1, keepdims=True)
        spread = jnp.sum(center * center, axis=-1, keepdims=True)
        value = center * lax.rsqrt(spread + 1e-06 * channels) * gain + bias
        dst[start : start + count, 0:channels] = value.astype(jnp.bfloat16)
        start += count


def mlp(w_aug_ref, w_out_ref, vectors, pad_ref, out_ref, segments, src):
    out_scale, out_bias = vectors
    side = out_ref.shape[1]
    z = jnp.dot(src[...], w_aug_ref[...], preferred_element_type=jnp.float32)
    act = (z + z * lax.erf(z)).astype(jnp.bfloat16)
    mixed = jnp.dot(act, w_out_ref[...], preferred_element_type=jnp.float32)
    mixed = mixed * out_scale + out_bias
    start = 0
    for tile, row, col, count in segments:
        line = tile * (side + 2) + row + 1
        old = pad_ref[line, pl.ds(OFF + col, count), :]
        new = old + mixed[start : start + count]
        out_ref[tile, row, pl.ds(col, count), :] = new.astype(out_ref.dtype)
        start += count


def vectors_of(dw_ref, dw_bias_ref, gain_ref, bias_ref, b_out_ref, scale_ref):
    channels = dw_ref.shape[1]
    taps = [dw_ref[k : k + 1] for k in range(9)]
    gain = gain_ref[...] * (ROOT_HALF * channels**0.5)
    first = (dw_bias_ref[...], gain, bias_ref[...] * ROOT_HALF)
    last = (scale_ref[...] * ROOT_HALF, scale_ref[...] * b_out_ref[...])
    return taps, first, last


def fill_ones(buf):
    rows, both = buf.shape
    lane = lax.broadcasted_iota(jnp.int32, (rows, both // 2), 1)
    buf[:, both // 2 :] = jnp.where(lane < 2, 1.0, 0.0).astype(jnp.bfloat16)


def last_flagged(flags, values):
    found = [jnp.int32(0)] * CROSS
    for flag, value in zip(flags, values):
        for k in range(CROSS - 1, 0, -1):
            found[k] = jnp.where(flag, found[k - 1], found[k])
        found[0] = jnp.where(flag, value, found[0])
    return found


def owned(partner, device, edges):
    local = partner - device * edges
    return (local >= 0) & (local < edges), local


def inner_kernel(
    sizes,
    partner_ref,
    cells_ref,
    dw_ref,
    dw_bias_ref,
    gain_ref,
    bias_ref,
    w_in_ref,
    b_in_ref,
    w_out_ref,
    b_out_ref,
    scale_ref,
    out_ref,
    pad_ref,
    rims_ref,
    recv_ref,
    w_aug_ref,
    cells_buf,
    send_buf,
    buf_a,
    buf_b,
    load_sem,
    send_sem,
    recv_sem,
):
    tile_devices, hidden_devices = sizes
    tiles, side, _, channels = out_ref.shape
    edges = 4 * tiles
    width = side + 2 * OFF
    devices = tile_devices * hidden_devices
    me = lax.axis_index("tile") * hidden_devices + lax.axis_index("hidden")

    def at(position):
        return (position // hidden_devices, position % hidden_devices)

    right = lax.rem(me + 1, devices)
    left = lax.rem(me + devices - 1, devices)
    loads = [
        pltpu.make_async_copy(cells_ref.at[t], cells_buf.at[t], load_sem.at[t])
        for t in range(tiles)
    ]
    for copy in loads:
        copy.start()
    barrier = pltpu.get_barrier_semaphore()
    for neighbour in (left, right):
        pl.semaphore_signal(barrier, inc=1, device_id=at(neighbour), device_id_type=MESH)

    partners = [partner_ref[e // 4, e % 4] for e in range(edges)]
    local = [jnp.int32(e) for e in range(edges)]
    going = []
    for device in (right, left):
        going += last_flagged([owned(p, device, edges)[0] for p in partners], local)

    flat_pad = pad_ref.reshape(tiles * (side + 2) * width, channels)
    for t in range(tiles):
        loads[t].wait()
        top = t * (side + 2)
        pad_ref[pl.ds(top + 1, side), pl.ds(OFF, side), :] = cells_buf[t].astype(jnp.float32)
        first = (top + 1) * width + OFF
        mine = 4 * t
        rims_ref[mine] = cells_buf[t, 0]
        rims_ref[mine + 2] = cells_buf[t, side - 1]
        east = flat_pad[pl.ds(first + side - 1, side, stride=width), :]
        rims_ref[mine + 1] = east.astype(jnp.bfloat16)
        west = flat_pad[pl.ds(first, side, stride=width), :]
        rims_ref[mine + 3] = west.astype(jnp.bfloat16)
    for k in range(2 * CROSS):
        send_buf[k] = rims_ref[going[k]]

    pl.semaphore_wait(barrier, 2)
    sends = [
        pltpu.make_async_remote_copy(
            src_ref=send_buf.at[pl.ds(side_id * CROSS, CROSS)],
            dst_ref=recv_ref.at[pl.ds(side_id * CROSS, CROSS)],
            send_sem=send_sem.at[side_id],
            recv_sem=recv_sem.at[side_id],
            device_id=at(target),
            device_id_type=MESH,
        )
        for side_id, target in ((0, right), (1, left))
    ]
    for copy in sends:
        copy.start()

    hidden = w_in_ref.shape[0]
    eye = (
        lax.broadcasted_iota(jnp.int32, (channels, channels), 0)
        == lax.broadcasted_iota(jnp.int32, (channels, channels), 1)
    ).astype(jnp.bfloat16)
    w_aug_ref[0:channels, :] = lax.dot_general(
        eye, w_in_ref[...], (((1,), (1,)), ((), ())), preferred_element_type=jnp.float32
    ).astype(jnp.bfloat16)
    b_in = b_in_ref[...].astype(jnp.float32).reshape(1, hidden) * ROOT_HALF
    b_high = b_in.astype(jnp.bfloat16).astype(jnp.float32)
    row_id = lax.broadcasted_iota(jnp.int32, (channels, hidden), 0)
    extra = jnp.where(row_id == 0, b_high, jnp.where(row_id == 1, b_in - b_high, 0.0))
    w_aug_ref[channels : 2 * channels, :] = extra.astype(jnp.bfloat16)
    fill_ones(buf_a)
    fill_ones(buf_b)

    taps, first, last = vectors_of(
        dw_ref, dw_bias_ref, gain_ref, bias_ref, b_out_ref, scale_ref
    )
    do_conv = functools.partial(conv, taps, first, pad_ref, side)
    do_mlp = functools.partial(mlp, w_aug_ref, w_out_ref, last, pad_ref, out_ref)
    inner_cols = side - 2 * OFF
    inner_rows = side - 2
    rows_in = CELLS_PER_CHUNK // inner_cols

    def inner(chunk):
        found = []
        for k in range(rows_in):
            q = chunk * rows_in + k
            tile = tile_of(q, inner_rows, tiles)
            found.append((tile, q - inner_rows * tile + 1, OFF, inner_cols))
        return found

    chunks = tiles * inner_rows // rows_in
    bufs = (buf_a, buf_b)
    do_conv(inner(0), buf_a)

    @pl.loop(0, (chunks - 1) // UNROLL)
    def _(i):
        for u in range(UNROLL):
            do_mlp(inner(UNROLL * i + u), bufs[u % 2])
            do_conv(inner(UNROLL * i + u + 1), bufs[(u + 1) % 2])

    for c in range((chunks - 1) // UNROLL * UNROLL, chunks):
        do_mlp(inner(c), bufs[c % 2])
        if c + 1 < chunks:
            do_conv(inner(c + 1), bufs[(c + 1) % 2])
    for copy in sends:
        copy.wait()


def edge_kernel(
    sizes,
    partner_ref,
    flip_ref,
    inner_ref,
    pad_in_ref,
    rims_ref,
    recv_ref,
    w_aug_ref,
    dw_ref,
    dw_bias_ref,
    gain_ref,
    bias_ref,
    w_out_ref,
    b_out_ref,
    scale_ref,
    out_hbm,
    pad_ref,
    out_ref,
    buf_a,
    buf_b,
    inner_sem,
    store_sem,
):
    tile_devices, hidden_devices = sizes
    tiles, side, _, channels = out_ref.shape
    edges = 4 * tiles
    width = side + 2 * OFF
    devices = tile_devices * hidden_devices
    inner_cols = side - 2 * OFF
    me = lax.axis_index("tile") * hidden_devices + lax.axis_index("hidden")
    right = lax.rem(me + 1, devices)
    left = lax.rem(me + devices - 1, devices)

    def piece(t, rows, first_row, cols, first_col):
        return (t, pl.ds(first_row, rows), pl.ds(first_col, cols))

    inner_copies = []
    for t in range(tiles):
        part = piece(t, side - 2, 1, inner_cols, OFF)
        inner_copies.append(
            pltpu.make_async_copy(inner_ref.at[part], out_hbm.at[part], inner_sem.at[t])
        )
    for copy in inner_copies:
        copy.start()

    partners = [partner_ref[e // 4, e % 4] for e in range(edges)]
    prev_flags, prev_local = zip(*[owned(p, left, edges) for p in partners])
    next_flags, next_local = zip(*[owned(p, right, edges) for p in partners])
    prev_list = last_flagged(prev_flags, prev_local)
    next_list = last_flagged(next_flags, next_local)

    def above(values, limit):
        return sum(jnp.where(value > limit, 1, 0) for value in values)

    flat_pad = pad_ref.reshape(tiles * (side + 2) * width, channels)
    r_id = lax.broadcasted_iota(jnp.int32, (side, side), 0)
    c_id = lax.broadcasted_iota(jnp.int32, (side, side), 1)
    for t in range(tiles):
        lines = []
        for s in range(4):
            e = 4 * t + s
            is_prev, is_next = prev_flags[e], next_flags[e]
            slot = jnp.where(
                is_prev,
                above(prev_list, prev_local[e]),
                CROSS + above(next_list, next_local[e]),
            )
            crosses = is_prev | is_next
            own_edge = jnp.where(crosses, 0, partners[e] - me * edges)
            received = recv_ref[jnp.where(crosses, slot, 0)]
            line = jnp.where(crosses, received, rims_ref[own_edge])
            target = jnp.where(flip_ref[t, s] == 1, side - 1 - r_id, r_id)
            order = jnp.where(c_id == target, 1.0, 0.0).astype(jnp.bfloat16)
            lines.append(jnp.dot(order, line, preferred_element_type=jnp.float32))
        north, east, south, west = lines
        top = t * (side + 2)
        end = top + side + 1
        pad_ref[top, pl.ds(OFF, side), :] = north
        pad_ref[end, pl.ds(OFF, side), :] = south
        first = (top + 1) * width + OFF
        flat_pad[pl.ds(first - 1, side, stride=width), :] = west
        flat_pad[pl.ds(first + side, side, stride=width), :] = east
        pad_ref[top, OFF - 1 : OFF, :] = 0.5 * (north[:1] + west[:1])
        pad_ref[top, OFF + side : OFF + side + 1, :] = 0.5 * (north[-1:] + east[:1])
        pad_ref[end, OFF - 1 : OFF, :] = 0.5 * (south[:1] + west[-1:])
        pad_ref[end, OFF + side : OFF + side + 1, :] = 0.5 * (south[-1:] + east[-1:])

    fill_ones(buf_a)
    fill_ones(buf_b)
    taps, first, last = vectors_of(
        dw_ref, dw_bias_ref, gain_ref, bias_ref, b_out_ref, scale_ref
    )
    do_conv = functools.partial(conv, taps, first, pad_ref, side)
    do_mlp = functools.partial(mlp, w_aug_ref, w_out_ref, last, pad_ref, out_ref)
    caps = [(t, r, OFF, inner_cols) for t in range(tiles) for r in (0, side - 1)]
    rows_edge = CELLS_PER_CHUNK // (2 * OFF)
    per_tile = side // rows_edge

    def sides(chunk):
        found = []
        for k in range(rows_edge):
            tile = chunk // per_tile
            row = (chunk % per_tile) * rows_edge + k
            found += [(tile, row, 0, OFF), (tile, row, side - OFF, OFF)]
        return found

    chunks = tiles * per_tile
    stores = []
    for t in range(tiles):
        for n, part in enumerate(
            (
                piece(t, 1, 0, side, 0),
                piece(t, 1, side - 1, side, 0),
                piece(t, side - 2, 1, OFF, 0),
                piece(t, side - 2, 1, OFF, side - OFF),
            )
        ):
            stores.append(
                pltpu.make_async_copy(out_ref.at[part], out_hbm.at[part], store_sem.at[t, n])
            )
    do_conv(caps, buf_b)
    do_mlp(caps, buf_b)
    do_conv(sides(0), buf_a)

    @pl.loop(0, chunks // 2 - 1)
    def _(i):
        do_mlp(sides(2 * i), buf_a)
        do_conv(sides(2 * i + 1), buf_b)
        do_mlp(sides(2 * i + 1), buf_b)
        do_conv(sides(2 * i + 2), buf_a)

    do_mlp(sides(chunks - 2), buf_a)
    do_conv(sides(chunks - 1), buf_b)
    do_mlp(sides(chunks - 1), buf_b)
    for copy in stores:
        copy.start()
    for copy in inner_copies + stores:
        copy.wait()


def per_device(
    sizes,
    cells,
    partner_edge,
    edge_flip,
    dw_weight,
    dw_bias,
    ln_gain,
    ln_bias,
    w_in,
    b_in,
    w_out,
    b_out,
    layer_scale,
):
    tiles, side, _, channels = cells.shape
    hidden = w_in.shape[0]
    edges = 4 * tiles
    vmem = pl.BlockSpec(memory_space=pltpu.VMEM)
    smem = pl.BlockSpec(memory_space=pltpu.SMEM)
    anywhere = pl.BlockSpec(memory_space=pltpu.HBM)
    dw_bias, ln_gain, ln_bias, b_out, layer_scale = (
        vector.reshape(1, channels)
        for vector in (dw_bias, ln_gain, ln_bias, b_out, layer_scale)
    )
    pad_shape = (tiles * (side + 2), side + 2 * OFF, channels)
    buffers = [pltpu.VMEM((CELLS_PER_CHUNK, 2 * channels), jnp.bfloat16)] * 2
    inner, pad, rims, recv, w_aug = pl.pallas_call(
        functools.partial(inner_kernel, sizes),
        out_shape=(
            pltpu.VMEM(cells.shape, jnp.bfloat16),
            pltpu.VMEM(pad_shape, jnp.float32),
            pltpu.VMEM((edges, side, channels), jnp.bfloat16),
            pltpu.VMEM((2 * CROSS, side, channels), jnp.bfloat16),
            pltpu.VMEM((2 * channels, hidden), jnp.bfloat16),
        ),
        in_specs=[smem, anywhere] + [vmem] * 9,
        out_specs=(vmem,) * 5,
        scratch_shapes=[
            pltpu.VMEM(cells.shape, jnp.bfloat16),
            pltpu.VMEM((2 * CROSS, side, channels), jnp.bfloat16),
            *buffers,
            pltpu.SemaphoreType.DMA((tiles,)),
            pltpu.SemaphoreType.DMA((2,)),
            pltpu.SemaphoreType.DMA((2,)),
        ],
        compiler_params=pltpu.CompilerParams(
            collective_id=0, has_side_effects=True, vmem_limit_bytes=GRANT
        ),
        name="inner",
    )(
        partner_edge,
        cells,
        dw_weight,
        dw_bias,
        ln_gain,
        ln_bias,
        w_in,
        b_in,
        w_out,
        b_out,
        layer_scale,
    )
    return pl.pallas_call(
        functools.partial(edge_kernel, sizes),
        out_shape=(
            jax.ShapeDtypeStruct(cells.shape, jnp.bfloat16),
            pltpu.VMEM(pad_shape, jnp.float32),
        ),
        in_specs=[smem, smem] + [vmem] * 12,
        out_specs=(anywhere, vmem),
        input_output_aliases={3: 1},
        scratch_shapes=[
            pltpu.VMEM(cells.shape, jnp.bfloat16),
            *buffers,
            pltpu.SemaphoreType.DMA((tiles,)),
            pltpu.SemaphoreType.DMA((tiles, 4)),
        ],
        compiler_params=pltpu.CompilerParams(vmem_limit_bytes=GRANT),
        name="edge",
    )(
        partner_edge,
        edge_flip,
        inner,
        pad,
        rims,
        recv,
        w_aug,
        dw_weight,
        dw_bias,
        ln_gain,
        ln_bias,
        w_out,
        b_out,
        layer_scale,
    )[0]


def solution(mesh):
    spread_spec = P(AXES, None, None, None)
    in_specs = (spread_spec, P(AXES, None), P(AXES, None)) + (P(),) * 9
    sizes = (mesh.shape["tile"], mesh.shape["hidden"])
    return jax.shard_map(
        functools.partial(per_device, sizes),
        mesh=mesh,
        in_specs=in_specs,
        out_specs=spread_spec,
        check_vma=False,
    )
```

```python
import functools

import jax
import jax.numpy as jnp
from jax import lax
from jax.experimental import pallas as pl
from jax.experimental.pallas import tpu as pltpu
from jax.sharding import PartitionSpec as P

AXES = ("tile", "hidden")
OFF = 8
CELLS_PER_CHUNK = 256
UNROLL = 4
CROSS = 4
GRANT = 32 * 1024 * 1024
MESH = pl.DeviceIdType.MESH
ROOT_HALF = 0.7071067811865476


def tile_of(q, per_tile, tiles):
    tile = 0
    for j in range(1, tiles):
        tile = tile + jnp.where(q >= j * per_tile, 1, 0)
    return tile


def conv(taps, vectors, pad_ref, side, segments, dst):
    dw_bias, gain, bias = vectors
    channels = pad_ref.shape[2]
    start = 0
    for tile, row, col, count in segments:
        line = tile * (side + 2) + row
        total = jnp.broadcast_to(dw_bias, (count, channels))
        for a in range(3):
            for b in range(3):
                total = total + taps[3 * a + b] * pad_ref[
                    line + a, pl.ds(OFF - 1 + b + col, count), :
                ]
        center = total - jnp.mean(total, axis=-1, keepdims=True)
        spread = jnp.sum(center * center, axis=-1, keepdims=True)
        value = center * lax.rsqrt(spread + 1e-06 * channels) * gain + bias
        dst[start : start + count, 0:channels] = value.astype(jnp.bfloat16)
        start += count


def mlp(w_aug_ref, w_out_ref, vectors, pad_ref, out_ref, segments, src):
    out_scale, out_bias = vectors
    side = out_ref.shape[1]
    z = jnp.dot(src[...], w_aug_ref[...], preferred_element_type=jnp.float32)
    act = (z + z * lax.erf(z)).astype(jnp.bfloat16)
    mixed = jnp.dot(act, w_out_ref[...], preferred_element_type=jnp.float32)
    mixed = mixed * out_scale + out_bias
    start = 0
    for tile, row, col, count in segments:
        line = tile * (side + 2) + row + 1
        old = pad_ref[line, pl.ds(OFF + col, count), :]
        new = old + mixed[start : start + count]
        out_ref[tile, row, pl.ds(col, count), :] = new.astype(out_ref.dtype)
        start += count


def vectors_of(dw_ref, dw_bias_ref, gain_ref, bias_ref, b_out_ref, scale_ref):
    channels = dw_ref.shape[1]
    taps = [dw_ref[k : k + 1] for k in range(9)]
    gain = gain_ref[...] * (ROOT_HALF * channels**0.5)
    first = (dw_bias_ref[...], gain, bias_ref[...] * ROOT_HALF)
    last = (scale_ref[...] * ROOT_HALF, scale_ref[...] * b_out_ref[...])
    return taps, first, last


def fill_ones(buf):
    rows, both = buf.shape
    lane = lax.broadcasted_iota(jnp.int32, (rows, both // 2), 1)
    buf[:, both // 2 :] = jnp.where(lane < 2, 1.0, 0.0).astype(jnp.bfloat16)


def last_flagged(flags, values):
    found = [jnp.int32(0)] * CROSS
    for flag, value in zip(flags, values):
        for k in range(CROSS - 1, 0, -1):
            found[k] = jnp.where(flag, found[k - 1], found[k])
        found[0] = jnp.where(flag, value, found[0])
    return found


def owned(partner, device, edges):
    local = partner - device * edges
    return (local >= 0) & (local < edges), local


def inner_kernel(
    sizes,
    partner_ref,
    cells_ref,
    dw_ref,
    dw_bias_ref,
    gain_ref,
    bias_ref,
    w_in_ref,
    b_in_ref,
    w_out_ref,
    b_out_ref,
    scale_ref,
    out_ref,
    pad_ref,
    rims_ref,
    recv_ref,
    w_aug_ref,
    cells_buf,
    send_buf,
    buf_a,
    buf_b,
    load_sem,
    send_sem,
    recv_sem,
):
    tile_devices, hidden_devices = sizes
    tiles, side, _, channels = out_ref.shape
    edges = 4 * tiles
    width = side + 2 * OFF
    devices = tile_devices * hidden_devices
    me = lax.axis_index("tile") * hidden_devices + lax.axis_index("hidden")

    def at(position):
        return (position // hidden_devices, position % hidden_devices)

    right = lax.rem(me + 1, devices)
    left = lax.rem(me + devices - 1, devices)
    loads = [
        pltpu.make_async_copy(cells_ref.at[t], cells_buf.at[t], load_sem.at[t])
        for t in range(tiles)
    ]
    for copy in loads:
        copy.start()
    barrier = pltpu.get_barrier_semaphore()
    for neighbour in (left, right):
        pl.semaphore_signal(barrier, inc=1, device_id=at(neighbour), device_id_type=MESH)

    partners = [partner_ref[e // 4, e % 4] for e in range(edges)]
    local = [jnp.int32(e) for e in range(edges)]
    going = []
    for device in (right, left):
        going += last_flagged([owned(p, device, edges)[0] for p in partners], local)

    flat_pad = pad_ref.reshape(tiles * (side + 2) * width, channels)
    for t in range(tiles):
        loads[t].wait()
        top = t * (side + 2)
        pad_ref[pl.ds(top + 1, side), pl.ds(OFF, side), :] = cells_buf[t].astype(jnp.float32)
        first = (top + 1) * width + OFF
        mine = 4 * t
        rims_ref[mine] = cells_buf[t, 0]
        rims_ref[mine + 2] = cells_buf[t, side - 1]
        east = flat_pad[pl.ds(first + side - 1, side, stride=width), :]
        rims_ref[mine + 1] = east.astype(jnp.bfloat16)
        west = flat_pad[pl.ds(first, side, stride=width), :]
        rims_ref[mine + 3] = west.astype(jnp.bfloat16)
    for k in range(2 * CROSS):
        send_buf[k] = rims_ref[going[k]]

    pl.semaphore_wait(barrier, 2)
    sends = [
        pltpu.make_async_remote_copy(
            src_ref=send_buf.at[pl.ds(side_id * CROSS, CROSS)],
            dst_ref=recv_ref.at[pl.ds(side_id * CROSS, CROSS)],
            send_sem=send_sem.at[side_id],
            recv_sem=recv_sem.at[side_id],
            device_id=at(target),
            device_id_type=MESH,
        )
        for side_id, target in ((0, right), (1, left))
    ]
    for copy in sends:
        copy.start()

    hidden = w_in_ref.shape[0]
    eye = (
        lax.broadcasted_iota(jnp.int32, (channels, channels), 0)
        == lax.broadcasted_iota(jnp.int32, (channels, channels), 1)
    ).astype(jnp.bfloat16)
    w_aug_ref[0:channels, :] = lax.dot_general(
        eye, w_in_ref[...], (((1,), (1,)), ((), ())), preferred_element_type=jnp.float32
    ).astype(jnp.bfloat16)
    b_in = b_in_ref[...].astype(jnp.float32).reshape(1, hidden) * ROOT_HALF
    b_high = b_in.astype(jnp.bfloat16).astype(jnp.float32)
    row_id = lax.broadcasted_iota(jnp.int32, (channels, hidden), 0)
    extra = jnp.where(row_id == 0, b_high, jnp.where(row_id == 1, b_in - b_high, 0.0))
    w_aug_ref[channels : 2 * channels, :] = extra.astype(jnp.bfloat16)
    fill_ones(buf_a)
    fill_ones(buf_b)

    taps, first, last = vectors_of(
        dw_ref, dw_bias_ref, gain_ref, bias_ref, b_out_ref, scale_ref
    )
    do_conv = functools.partial(conv, taps, first, pad_ref, side)
    do_mlp = functools.partial(mlp, w_aug_ref, w_out_ref, last, pad_ref, out_ref)
    inner_cols = side - 2 * OFF
    inner_rows = side - 2
    rows_in = CELLS_PER_CHUNK // inner_cols

    def inner(chunk):
        found = []
        for k in range(rows_in):
            q = chunk * rows_in + k
            tile = tile_of(q, inner_rows, tiles)
            found.append((tile, q - inner_rows * tile + 1, OFF, inner_cols))
        return found

    chunks = tiles * inner_rows // rows_in
    bufs = (buf_a, buf_b)
    do_conv(inner(0), buf_a)

    @pl.loop(0, (chunks - 1) // UNROLL)
    def _(i):
        for u in range(UNROLL):
            do_mlp(inner(UNROLL * i + u), bufs[u % 2])
            do_conv(inner(UNROLL * i + u + 1), bufs[(u + 1) % 2])

    for c in range((chunks - 1) // UNROLL * UNROLL, chunks):
        do_mlp(inner(c), bufs[c % 2])
        if c + 1 < chunks:
            do_conv(inner(c + 1), bufs[(c + 1) % 2])
    for copy in sends:
        copy.wait()


def edge_kernel(
    sizes,
    partner_ref,
    flip_ref,
    inner_ref,
    pad_in_ref,
    rims_ref,
    recv_ref,
    w_aug_ref,
    dw_ref,
    dw_bias_ref,
    gain_ref,
    bias_ref,
    w_out_ref,
    b_out_ref,
    scale_ref,
    out_hbm,
    pad_ref,
    out_ref,
    buf_a,
    buf_b,
    inner_sem,
    store_sem,
):
    tile_devices, hidden_devices = sizes
    tiles, side, _, channels = out_ref.shape
    edges = 4 * tiles
    width = side + 2 * OFF
    devices = tile_devices * hidden_devices
    inner_cols = side - 2 * OFF
    me = lax.axis_index("tile") * hidden_devices + lax.axis_index("hidden")
    right = lax.rem(me + 1, devices)
    left = lax.rem(me + devices - 1, devices)

    def piece(t, rows, first_row, cols, first_col):
        return (t, pl.ds(first_row, rows), pl.ds(first_col, cols))

    inner_copies = []
    for t in range(tiles):
        part = piece(t, side - 2, 1, inner_cols, OFF)
        inner_copies.append(
            pltpu.make_async_copy(inner_ref.at[part], out_hbm.at[part], inner_sem.at[t])
        )
    for copy in inner_copies:
        copy.start()

    partners = [partner_ref[e // 4, e % 4] for e in range(edges)]
    prev_flags, prev_local = zip(*[owned(p, left, edges) for p in partners])
    next_flags, next_local = zip(*[owned(p, right, edges) for p in partners])
    prev_list = last_flagged(prev_flags, prev_local)
    next_list = last_flagged(next_flags, next_local)

    def above(values, limit):
        return sum(jnp.where(value > limit, 1, 0) for value in values)

    flat_pad = pad_ref.reshape(tiles * (side + 2) * width, channels)
    r_id = lax.broadcasted_iota(jnp.int32, (side, side), 0)
    c_id = lax.broadcasted_iota(jnp.int32, (side, side), 1)
    for t in range(tiles):
        lines = []
        for s in range(4):
            e = 4 * t + s
            is_prev, is_next = prev_flags[e], next_flags[e]
            slot = jnp.where(
                is_prev,
                above(prev_list, prev_local[e]),
                CROSS + above(next_list, next_local[e]),
            )
            crosses = is_prev | is_next
            own_edge = jnp.where(crosses, 0, partners[e] - me * edges)
            received = recv_ref[jnp.where(crosses, slot, 0)]
            line = jnp.where(crosses, received, rims_ref[own_edge])
            target = jnp.where(flip_ref[t, s] == 1, side - 1 - r_id, r_id)
            order = jnp.where(c_id == target, 1.0, 0.0).astype(jnp.bfloat16)
            lines.append(jnp.dot(order, line, preferred_element_type=jnp.float32))
        north, east, south, west = lines
        top = t * (side + 2)
        end = top + side + 1
        pad_ref[top, pl.ds(OFF, side), :] = north
        pad_ref[end, pl.ds(OFF, side), :] = south
        first = (top + 1) * width + OFF
        flat_pad[pl.ds(first - 1, side, stride=width), :] = west
        flat_pad[pl.ds(first + side, side, stride=width), :] = east
        pad_ref[top, OFF - 1 : OFF, :] = 0.5 * (north[:1] + west[:1])
        pad_ref[top, OFF + side : OFF + side + 1, :] = 0.5 * (north[-1:] + east[:1])
        pad_ref[end, OFF - 1 : OFF, :] = 0.5 * (south[:1] + west[-1:])
        pad_ref[end, OFF + side : OFF + side + 1, :] = 0.5 * (south[-1:] + east[-1:])

    fill_ones(buf_a)
    fill_ones(buf_b)
    taps, first, last = vectors_of(
        dw_ref, dw_bias_ref, gain_ref, bias_ref, b_out_ref, scale_ref
    )
    do_conv = functools.partial(conv, taps, first, pad_ref, side)
    do_mlp = functools.partial(mlp, w_aug_ref, w_out_ref, last, pad_ref, out_ref)
    caps = [(t, r, OFF, inner_cols) for t in range(tiles) for r in (0, side - 1)]
    rows_edge = CELLS_PER_CHUNK // (2 * OFF)
    per_tile = side // rows_edge

    def sides(chunk):
        found = []
        for k in range(rows_edge):
            tile = chunk // per_tile
            row = (chunk % per_tile) * rows_edge + k
            found += [(tile, row, 0, OFF), (tile, row, side - OFF, OFF)]
        return found

    chunks = tiles * per_tile
    stores = []
    for t in range(tiles):
        for n, part in enumerate(
            (
                piece(t, 1, 0, side, 0),
                piece(t, 1, side - 1, side, 0),
                piece(t, side - 2, 1, OFF, 0),
                piece(t, side - 2, 1, OFF, side - OFF),
            )
        ):
            stores.append(
                pltpu.make_async_copy(out_ref.at[part], out_hbm.at[part], store_sem.at[t, n])
            )
    do_conv(caps, buf_b)
    do_mlp(caps, buf_b)
    do_conv(sides(0), buf_a)

    @pl.loop(0, chunks // 2 - 1)
    def _(i):
        do_mlp(sides(2 * i), buf_a)
        do_conv(sides(2 * i + 1), buf_b)
        do_mlp(sides(2 * i + 1), buf_b)
        do_conv(sides(2 * i + 2), buf_a)

    do_mlp(sides(chunks - 2), buf_a)
    do_conv(sides(chunks - 1), buf_b)
    do_mlp(sides(chunks - 1), buf_b)
    for copy in stores:
        copy.start()
    for copy in inner_copies + stores:
        copy.wait()


def per_device(
    sizes,
    cells,
    partner_edge,
    edge_flip,
    dw_weight,
    dw_bias,
    ln_gain,
    ln_bias,
    w_in,
    b_in,
    w_out,
    b_out,
    layer_scale,
):
    tiles, side, _, channels = cells.shape
    hidden = w_in.shape[0]
    edges = 4 * tiles
    vmem = pl.BlockSpec(memory_space=pltpu.VMEM)
    smem = pl.BlockSpec(memory_space=pltpu.SMEM)
    anywhere = pl.BlockSpec(memory_space=pltpu.HBM)
    dw_bias, ln_gain, ln_bias, b_out, layer_scale = (
        vector.reshape(1, channels)
        for vector in (dw_bias, ln_gain, ln_bias, b_out, layer_scale)
    )
    (
        cells,
        partner_edge,
        edge_flip,
        dw_weight,
        dw_bias,
        ln_gain,
        ln_bias,
        w_in,
        b_in,
        w_out,
        b_out,
        layer_scale,
    ) = (
        pltpu.with_memory_space_constraint(array, pltpu.HBM)
        for array in (
            cells,
            partner_edge,
            edge_flip,
            dw_weight,
            dw_bias,
            ln_gain,
            ln_bias,
            w_in,
            b_in,
            w_out,
            b_out,
            layer_scale,
        )
    )
    pad_shape = (tiles * (side + 2), side + 2 * OFF, channels)
    buffers = [pltpu.VMEM((CELLS_PER_CHUNK, 2 * channels), jnp.bfloat16)] * 2
    inner, pad, rims, recv, w_aug = pl.pallas_call(
        functools.partial(inner_kernel, sizes),
        out_shape=(
            pltpu.VMEM(cells.shape, jnp.bfloat16),
            pltpu.VMEM(pad_shape, jnp.float32),
            pltpu.VMEM((edges, side, channels), jnp.bfloat16),
            pltpu.VMEM((2 * CROSS, side, channels), jnp.bfloat16),
            pltpu.VMEM((2 * channels, hidden), jnp.bfloat16),
        ),
        in_specs=[smem, anywhere] + [vmem] * 9,
        out_specs=(vmem,) * 5,
        scratch_shapes=[
            pltpu.VMEM(cells.shape, jnp.bfloat16),
            pltpu.VMEM((2 * CROSS, side, channels), jnp.bfloat16),
            *buffers,
            pltpu.SemaphoreType.DMA((tiles,)),
            pltpu.SemaphoreType.DMA((2,)),
            pltpu.SemaphoreType.DMA((2,)),
        ],
        compiler_params=pltpu.CompilerParams(
            collective_id=0, has_side_effects=True, vmem_limit_bytes=GRANT
        ),
        name="inner",
    )(
        partner_edge,
        cells,
        dw_weight,
        dw_bias,
        ln_gain,
        ln_bias,
        w_in,
        b_in,
        w_out,
        b_out,
        layer_scale,
    )
    return pl.pallas_call(
        functools.partial(edge_kernel, sizes),
        out_shape=(
            jax.ShapeDtypeStruct(cells.shape, jnp.bfloat16),
            pltpu.VMEM(pad_shape, jnp.float32),
        ),
        in_specs=[smem, smem] + [vmem] * 12,
        out_specs=(anywhere, vmem),
        input_output_aliases={3: 1},
        scratch_shapes=[
            pltpu.VMEM(cells.shape, jnp.bfloat16),
            *buffers,
            pltpu.SemaphoreType.DMA((tiles,)),
            pltpu.SemaphoreType.DMA((tiles, 4)),
        ],
        compiler_params=pltpu.CompilerParams(vmem_limit_bytes=GRANT),
        name="edge",
    )(
        partner_edge,
        edge_flip,
        inner,
        pad,
        rims,
        recv,
        w_aug,
        dw_weight,
        dw_bias,
        ln_gain,
        ln_bias,
        w_out,
        b_out,
        layer_scale,
    )[0]


def solution(mesh):
    spread_spec = P(AXES, None, None, None)
    in_specs = (spread_spec, P(AXES, None), P(AXES, None)) + (P(),) * 9
    sizes = (mesh.shape["tile"], mesh.shape["hidden"])
    return jax.shard_map(
        functools.partial(per_device, sizes),
        mesh=mesh,
        in_specs=in_specs,
        out_specs=spread_spec,
        check_vma=False,
    )
```
